32 devices in a mesh: pb: 4 (over y, core), ma: 8 (over z, x).
Axes of the slice: x: 2, y: 2, z: 4, core: 2. Of those that a mesh axis runs over, the one named last changes fastest.
Arguments:
- queries: bfloat16 [1, 1024, 2048], P(None, ('pb', 'ma')), may hold values from -6 to 6
- map_descriptors: bfloat16 [8192, 2048], P('ma', 'pb'), may hold values from -0.125 to 0.125
- slopes: int32 [8], replicated, may hold values from 0 to 15, as said below
Outputs:
- best: float32 [1, 1024, 8192], P(None, 'pb', 'ma')
The draws below stay inside these ranges and needn't reach their ends.
Inputs may be any that keep to these rules, and one draw needn't show every extreme that they name: `slopes`: 8 distinct velocities; the largest is exactly 15.
All inputs are finite; a program needn't handle non-finite values.
Results may differ from the reference program's by a relative error of at most 0.0003.
Values may be sent and summed in bfloat16 or wider, within the bound.
A program may use at most 64 MiB of HBM per device.

```python
import math
import jax
import jax.numpy as jnp
from jax import lax

D = 2048
SESS = 1
SEQ = 20
RAD = 10
VMAX = 15
NSLOPE = 8
SPAN = 285
NQ = 1024
NM = 8192


def draw_slopes(key, part):
    order = jax.random.permutation(key, VMAX + 1)[:NSLOPE]
    largest = jnp.max(order)
    return jnp.where(order == largest, VMAX, order).astype(jnp.int32)


def steps_of(key, dims, cuts, smallest, high):
    factor_of = 1.0
    for axis_at, shards_of in cuts:
        heights = jax.random.uniform(jax.random.fold_in(jax.random.fold_in(key, 6), axis_at), (shards_of,), jnp.float32, smallest / len(cuts), high / len(cuts))
        factor_of = factor_of * jnp.repeat(jnp.exp(heights), dims[axis_at] // shards_of).reshape((-1,) + (1,) * (len(dims) - 1 - axis_at))
    return factor_of


def gaussian(key, dims, deviation, bound, cuts=(), held_as=jnp.bfloat16):
    result = jax.random.normal(key, dims, jnp.float32) * deviation
    if len(cuts) > 0:
        result = steps_of(key, dims, cuts, -0.22, 0.18) * result
    return jnp.clip(result, min=-bound, max=bound).astype(held_as)


def setup_inputs(seed: int = 0) -> dict:
    streams_of = jax.random.split(jax.random.key(seed), 4)
    return {
        "queries": gaussian(streams_of[0], (SESS, NQ, D), 1.0, 6.0, ((1, 32),)),
        "map_descriptors": gaussian(streams_of[1], (NM, D), D ** -0.5, 0.125, ((0, 8), (1, 4))),
        "slopes": draw_slopes(jax.random.fold_in(streams_of[3], 71), 0),
    }


def reference(queries, map_descriptors, slopes):

    def one_traversal(query_rows):
        scores = lax.dot_general(query_rows, map_descriptors, (((1,), (1,)), ((), ())), preferred_element_type=jnp.float32)
        padded = jnp.pad(scores, ((0, 0), (RAD, RAD)))
        running = jnp.zeros(scores.shape, jnp.float32)
        squares = jnp.zeros(scores.shape, jnp.float32)
        for offset in range(2 * RAD + 1):
            window = padded[:, offset:offset + NM]
            running = running + window
            squares = squares + window * window
        average = running / (2 * RAD + 1)
        spread = squares / (2 * RAD + 1) - average * average
        normal = (scores - average) / jnp.sqrt(spread + 1.0)
        normal_pad = jnp.pad(normal, ((SEQ - 1, 0), (SPAN, 0)))

        def per_slope(best_val, velocity):
            summed = jnp.zeros((NQ, NM), jnp.float32)
            for lag_step in range(SEQ):
                row_at = jnp.asarray(SEQ - 1 - lag_step, jnp.int32)
                col_at = (SPAN - lag_step * velocity).astype(jnp.int32)
                summed = summed + lax.dynamic_slice(normal_pad, (row_at, col_at), (NQ, NM))
            return (jnp.maximum(best_val, summed), None)
        start_best = jnp.full((NQ, NM), -jnp.inf, jnp.float32)
        best_val, unused = lax.scan(per_slope, start_best, slopes)
        return best_val / math.sqrt(SEQ)
    return lax.map(one_traversal, queries)
```

```python
import math

import jax
import jax.numpy as jnp
from jax import lax
from jax.experimental import pallas as pl
from jax.experimental.pallas import tpu as pltpu
from jax.sharding import PartitionSpec as P

MESH = pl.DeviceIdType.MESH
SEQ = 20
RAD = 10
LEAD = 32
LEFT = 384
RIGHT = 128
LANES = 128
CORES = 2


def remote(src, dst, send, recv, where):
    return pltpu.make_async_remote_copy(
        src_ref=src,
        dst_ref=dst,
        send_sem=send,
        recv_sem=recv,
        device_id=where,
        device_id_type=MESH,
    )


def coded(block, narrow=True):
    top = jnp.max(jnp.abs(block), axis=1, keepdims=True)
    power = jnp.ceil(jnp.log2(jnp.maximum(top, 1e-30)) + 1e-3)
    code = jnp.floor(block * jnp.exp2(15.0 - power) + 0.5)
    code = jnp.clip(code, -32767.0, 32767.0)
    tail = jnp.broadcast_to(power, (block.shape[0], LANES))
    code, tail = code.astype(jnp.int32), tail.astype(jnp.int32)
    return (code.astype(jnp.int16), tail.astype(jnp.int16)) if narrow else (code, tail)


def whole(code):
    return code.astype(jnp.int32).astype(jnp.float32)


def score_kernel(
    npb,
    nma,
    q_ref,
    m_ref,
    out_ref,
    q_all,
    m_all,
    p_out,
    p_in,
    r_out,
    l_out,
    l_in,
    r_in,
    local_sem,
    m_send,
    m_recv,
    y_send,
    y_recv,
    z_send,
    z_recv,
    x_send,
    x_recv,
    p_send,
    p_recv,
    halo_send,
    halo_recv,
    lead_send,
    lead_recv,
):
    pb, ma = lax.axis_index("pb"), lax.axis_index("ma")
    pair, across = npb // CORES, nma // 2
    row, core = pb // CORES, pb % CORES
    z, x = ma // 2, ma % 2
    each = q_all.shape[2]
    share = q_all.shape[3]
    m_count, half = m_ref.shape
    size = 2 * each
    last = across - 1
    mate = {"pb": row * CORES + 1 - core}
    twin = {"ma": z * 2 + 1 - x}
    block_of = [lax.rem(row + pair - k, pair) for k in range(pair)]
    row_at = [{"pb": lax.rem(row + k, pair) * CORES + core} for k in range(pair)]
    below, above = {"ma": ma - 2}, {"ma": ma + 2}
    has_below, has_above = z > 0, z < last
    has_up, has_down = pb > 0, pb < npb - 1
    has_left, has_right = ma > 0, ma < nma - 1

    barrier = pltpu.get_barrier_semaphore()

    def greet(where):
        pl.semaphore_signal(barrier, inc=1, device_id=where, device_id_type=MESH)

    greet(mate)
    greet(twin)
    for k in range(1, pair):
        greet(row_at[k])
    sides = (
        (has_above, above),
        (has_below, below),
        (has_left, {"ma": ma - 1}),
        (has_right, {"ma": ma + 1}),
        (has_up, {"pb": pb - 1}),
        (has_down, {"pb": pb + 1}),
        (has_up & has_left, {"pb": pb - 1, "ma": ma - 1}),
        (has_up & has_right, {"pb": pb - 1, "ma": ma + 1}),
        (has_down & has_left, {"pb": pb + 1, "ma": ma - 1}),
        (has_down & has_right, {"pb": pb + 1, "ma": ma + 1}),
    )
    for test, where in sides:

        @pl.when(test)
        def _():
            greet(where)

    extra = sum(jnp.where(test, 1, 0) for test, _ in sides)
    pl.semaphore_wait(barrier, pair + 1 + extra)

    def part(k):
        at = pl.multiple_of(lax.rem(row + k, pair) * share, LANES)
        return q_ref.at[0, :, pl.ds(at, share)]

    to_row = [None] + [
        remote(part(k), q_all.at[row, ma], y_send.at[k], y_recv.at[k], row_at[k])
        for k in range(1, pair)
    ]
    for copy in to_row[1:]:
        copy.start()
    load_q = pltpu.make_async_copy(part(0), q_all.at[row, ma], local_sem.at[0])
    load_q.start()
    to_mate = remote(m_ref, m_all.at[core], m_send.at[0], m_recv.at[0], mate)
    to_mate.start()
    load_m = pltpu.make_async_copy(m_ref, m_all.at[core], local_sem.at[1])
    load_m.start()

    def ranked(e):
        far = lax.div(e + 1, 2)
        there = z + jnp.where(lax.rem(e, 2) == 1, -far, far)
        return there, (there >= 0) & (there <= last)

    def block_at(k, there, column):
        return q_all.at[block_of[k], there * 2 + column]

    def along_z(k, there, number, where):
        block = block_at(k, there, x)
        return remote(block, block, z_send.at[k, number], z_recv.at[k, there], where)

    def along_x(k, there):
        block = block_at(k, there, x)
        return remote(block, block, x_send.at[k, there], x_recv.at[k, there], twin)

    def spread(k):
        along_x(k, z).start()

        @pl.when(has_above)
        def _():
            along_z(k, z, z, above).start()

        @pl.when(has_below)
        def _():
            along_z(k, z, across, below).start()

    def forward(k, e):
        there, known = ranked(e)

        @pl.when(known)
        def _():
            along_z(k, there, there, twin).wait_recv()
            along_x(k, there).start()

        @pl.when(known & (there < z) & has_above)
        def _():
            along_z(k, there, there, above).start()

        @pl.when(known & (there > z) & has_below)
        def _():
            along_z(k, there, there, below).start()

    def from_x(k, there):
        block = block_at(k, there, 1 - x)
        return remote(block, block, x_send.at[k, there], x_recv.at[k, there], twin)

    load_q.wait()
    spread(0)
    forward(0, 1)
    forward(0, 2)
    for k in range(1, pair):
        to_row[k].wait_recv()
        spread(k)

    load_m.wait()
    to_mate.wait_recv()

    @pl.when(pb == 0)
    def _():
        out_ref[pl.ds(0, LEAD), :] = jnp.zeros((LEAD, out_ref.shape[1]), jnp.float32)

    @pl.when(ma == 0)
    def _():
        out_ref[:, pl.ds(0, LEFT)] = jnp.zeros((out_ref.shape[0], LEFT), jnp.float32)

    @pl.when(ma == nma - 1)
    def _():
        out_ref[:, pl.ds(LEFT + m_count, RIGHT)] = jnp.zeros(
            (out_ref.shape[0], RIGHT), jnp.float32
        )

    def score(k, there):
        block = q_all[block_of[k], pl.ds(there * 2, 2)]
        if each % 16 == 0:
            block = block.reshape(size, share)
        else:
            block = block.astype(jnp.float32).reshape(size, share).astype(block.dtype)
        total = None
        for slot in range(CORES):
            term = lax.dot_general(
                block[:, slot * half : (slot + 1) * half],
                m_all[slot],
                (((1,), (1,)), ((), ())),
                preferred_element_type=jnp.float32,
            )
            total = term if total is None else total + term
        return total

    def partial(k, there):
        return remote(
            p_out.at[k - 1, there],
            p_in.at[k - 1, there],
            p_send.at[k - 1, there],
            p_recv.at[k - 1, there],
            row_at[pair - k],
        )

    def add_partials(e):
        there, known = ranked(e)
        for k in range(1, pair):

            @pl.when(known)
            def _():
                from_x(k, there).wait_recv()
                code, tail = coded(score(k, there))
                p_out[k - 1, there, :, pl.ds(0, m_count)] = code
                p_out[k - 1, there, :, pl.ds(m_count, LANES)] = tail
                partial(k, there).start()

    @pl.loop(0, across)
    def _(d):
        for e in (2 * d + 1, 2 * d + 2):
            for k in range(1, pair):
                forward(k, e)
        for e in (2 * d + 3, 2 * d + 4):
            forward(0, e)

        @pl.when(d > 0)
        def _():
            add_partials(2 * d - 1)

        add_partials(2 * d)

    lead_each = min(LEAD, size)
    lead_parts = LEAD // lead_each

    def halos(there):
        right = remote(
            r_out.at[there], l_in.at[there], halo_send.at[0, there], halo_recv.at[0, there],
            {"ma": ma + 1},
        )
        left = remote(
            l_out.at[there], r_in.at[there], halo_send.at[1, there], halo_recv.at[1, there],
            {"ma": ma - 1},
        )
        return (has_right, has_left, right), (has_left, has_right, left)

    def leads(number):
        there = across - lead_parts + number
        rows = pl.ds(size - lead_each, lead_each)
        into = pl.ds(number * lead_each, lead_each)
        slot = across + number
        down, up = has_down, has_up
        main = remote(
            out_ref.at[pl.ds(LEAD + (there + 1) * size - lead_each, lead_each), pl.ds(LEFT, m_count)],
            out_ref.at[into, pl.ds(LEFT, m_count)],
            lead_send.at[0, number], lead_recv.at[0, number], {"pb": pb + 1},
        )
        right = remote(
            r_out.at[there, rows], l_in.at[slot, pl.ds(0, lead_each)],
            lead_send.at[1, number], lead_recv.at[1, number], {"pb": pb + 1, "ma": ma + 1},
        )
        left = remote(
            l_out.at[there, rows], r_in.at[slot, pl.ds(0, lead_each)],
            lead_send.at[2, number], lead_recv.at[2, number], {"pb": pb + 1, "ma": ma - 1},
        )
        return (
            (down, up, main),
            (down & has_right, up & has_left, right),
            (down & has_left, up & has_right, left),
        )

    def start(group):
        for sends, _, copy in group:

            @pl.when(sends)
            def _():
                copy.start()

    def edged(block, spare):
        code, tail = coded(block, narrow=False)
        lane = lax.broadcasted_iota(jnp.int32, code.shape, 1)
        if code.shape[1] > LANES:
            tail = jnp.concatenate([tail] * (code.shape[1] // LANES), axis=1)
        return jnp.where((lane >= spare) & (lane < spare + 16), tail, code).astype(jnp.int16)

    def opened(code, spare):
        value = whole(code)
        return value * jnp.exp2(value[:, spare : spare + 1] - 15.0)

    @pl.loop(0, 2 * across - 1)
    def _(e):
        there, known = ranked(e)

        @pl.when(known)
        def _():
            from_x(0, there).wait_recv()
            total = score(0, there)
            for k in range(1, pair):
                partial(k, there).wait_recv()
                scale = jnp.exp2(whole(p_in[k - 1, there, :, pl.ds(m_count, LANES)]) - 15.0)
                code = whole(p_in[k - 1, there, :, pl.ds(0, m_count)])
                total = total + code * scale[:, :1]
            at = pl.multiple_of(LEAD + there * size, 8)
            out_ref[pl.ds(at, size), pl.ds(LEFT, m_count)] = total
            r_out[there] = edged(total[:, m_count - LEFT :], 0)
            l_out[there] = edged(total[:, :RIGHT], LANES - 16)
            start(halos(there))
            for number in range(lead_parts):

                @pl.when(there == across - lead_parts + number)
                def _():
                    start(leads(number))

    def finish(group):
        for sends, receives, copy in group:

            @pl.when(receives)
            def _():
                copy.wait_recv()

            @pl.when(sends)
            def _():
                copy.wait_send()

    def unpack(rows, slot, count):
        @pl.when(has_left)
        def _():
            out_ref[rows, pl.ds(0, LEFT)] = opened(l_in[slot, pl.ds(0, count)], 0)

        @pl.when(has_right)
        def _():
            out_ref[rows, pl.ds(LEFT + m_count, RIGHT)] = opened(
                r_in[slot, pl.ds(0, count)], LANES - 16
            )

    @pl.loop(0, 2 * across - 1)
    def _(e):
        there, known = ranked(e)

        @pl.when(known)
        def _():
            finish(halos(there))
            unpack(pl.ds(pl.multiple_of(LEAD + there * size, 8), size), there, size)
            for k in range(1, pair):
                partial(k, there).wait_send()
            for k in range(pair):
                along_x(k, there).wait_send()

        for k in range(pair):
            onward = ((there < z) & has_above) | ((there > z) & has_below)

            @pl.when(known & onward)
            def _():
                along_z(k, there, there, twin).wait_send()

    for number in range(lead_parts):
        finish(leads(number))

        @pl.when(has_up)
        def _():
            unpack(pl.ds(number * lead_each, lead_each), across + number, lead_each)

    for k in range(1, pair):
        to_row[k].wait_send()
    to_mate.wait_send()
    for k in range(pair):

        @pl.when(has_above)
        def _():
            along_z(k, z, z, above).wait_send()

        @pl.when(has_below)
        def _():
            along_z(k, z, across, below).wait_send()


def score_tile(queries, map_descriptors, npb, nma):
    each, width = queries.shape[1:]
    m_count, half = map_descriptors.shape
    q_count = each * nma
    pair, across = npb // CORES, nma // 2
    size = 2 * each
    parts = LEAD // min(LEAD, size)
    dma = pltpu.SemaphoreType.DMA
    return pl.pallas_call(
        lambda *refs: score_kernel(npb, nma, *refs),
        out_shape=jax.ShapeDtypeStruct(
            (LEAD + q_count, LEFT + m_count + RIGHT), jnp.float32
        ),
        in_specs=[pl.BlockSpec(memory_space=pl.ANY)] * 2,
        out_specs=pl.BlockSpec(memory_space=pltpu.VMEM),
        scratch_shapes=[
            pltpu.VMEM((pair, nma, each, width // pair), jnp.bfloat16),
            pltpu.VMEM((CORES, m_count, half), jnp.bfloat16),
            pltpu.VMEM((pair - 1, across, size, m_count + LANES), jnp.int16),
            pltpu.VMEM((pair - 1, across, size, m_count + LANES), jnp.int16),
            pltpu.VMEM((across, size, LEFT), jnp.int16),
            pltpu.VMEM((across, size, RIGHT), jnp.int16),
            pltpu.VMEM((across + parts, size, LEFT), jnp.int16),
            pltpu.VMEM((across + parts, size, RIGHT), jnp.int16),
            dma((2,)),
            dma((1,)),
            dma((1,)),
            dma((pair,)),
            dma((pair,)),
            dma((pair, across + 1)),
            dma((pair, across)),
            dma((pair, across)),
            dma((pair, across)),
            dma((pair - 1, across)),
            dma((pair - 1, across)),
            dma((2, across)),
            dma((2, across)),
            dma((3, across)),
            dma((3, across)),
        ],
        compiler_params=pltpu.CompilerParams(
            collective_id=0, has_side_effects=True, vmem_limit_bytes=61 << 20
        ),
        name="scores",
    )(queries, map_descriptors)


STEP = 5
AHEAD = 8
HALF = 64


def best_kernel(
    slopes_ref, ext_ref, out_ref, c_ref, u_ref, w_ref, b_ref, o_ref, f_ref, g_ref, *s_refs
):
    pb, ma = lax.axis_index("pb"), lax.axis_index("ma")
    rows, width = ext_ref.shape
    q_count, m_count = rows - LEAD, width - LEFT - RIGHT
    halo = LEFT // LANES
    tiles = halo + m_count // LANES
    size = 2 * RAD + 1
    offset = STEP * AHEAD - LEAD

    block = 2 * LANES

    def band_of(depth, width, lead):
        inner = lax.broadcasted_iota(jnp.int32, (depth, width), 0)
        outer = lax.broadcasted_iota(jnp.int32, (depth, width), 1)
        near = jnp.abs(inner - lead - outer) <= RAD
        return jnp.where(near, 1.0, 0.0).astype(jnp.bfloat16)

    def window(value, band):
        total = None
        for _ in range(3):
            part = value.astype(jnp.bfloat16)
            value = value - part.astype(jnp.float32)
            term = jnp.dot(part, band, preferred_element_type=jnp.float32)
            total = term if total is None else total + term
        return total * (1.0 / size)

    group = 96
    first_row = jnp.where(pb == 0, LEAD, 0)
    first_col = jnp.where(ma == 0, LEFT, 0)
    edge = band_of(block, LANES, 0)
    inside = band_of(2 * block, block, LANES)

    def contrast(at, tile, lead, count, band):
        begin = tile * LANES - lead
        value = ext_ref[pl.ds(at, group), pl.ds(begin, band.shape[0])]
        centre = value[:, lead : lead + count * LANES]
        average = window(value, band)
        spread = window(value * value, band) - average * average
        normal = (centre - average) * (
            lax.rsqrt(spread + 1.0) * (1.0 / math.sqrt(SEQ))
        )
        row = lax.broadcasted_iota(jnp.int32, normal.shape, 0) + at
        col = lax.broadcasted_iota(jnp.int32, normal.shape, 1) + tile * LANES
        seen = (row >= first_row) & (col >= first_col)
        normal = jnp.where(seen, normal, 0.0)
        for half in range(count):
            c_ref[tile + half, pl.ds(at + offset, group), :] = normal[
                :, half * LANES : (half + 1) * LANES
            ]

    @pl.loop(0, rows // group)
    def _(number):
        at = pl.multiple_of(number * group, 8)
        contrast(at, 0, 0, 1, edge)
        for tile in range(1, tiles, 2):
            contrast(at, tile, LANES, 2, inside)

    span = m_count // 2
    depth = LEFT + span
    for t in range(STEP):
        for tile in range(depth // LANES):
            both = [
                c_ref[h * span // LANES + tile, pl.ds(t, HALF, stride=STEP), :]
                for h in range(2)
            ]
            turned = jnp.transpose(jnp.concatenate(both, axis=0))
            at = pl.ds(tile * LANES, LANES)
            u_ref[t, at, :] = turned
            if t < STEP - 1:
                w_ref[t, at, :] = pltpu.roll(turned, SEQ // STEP, 1)

    b_ref[...] = jnp.full(b_ref.shape, -jnp.inf, jnp.float32)
    start = LEFT - 288, LEFT - 216, LEFT - 64, LEFT - 48, LEFT - 32, LEFT - 16, LEFT

    def vec(at):
        return pl.ds(at, 8)

    @pl.loop(0, slopes_ref.shape[0])
    def _(index):
        v = slopes_ref[index]
        for at in range(start[0], depth, 8):
            total = u_ref[STEP - 1, vec(at), :]
            for k in range(1, STEP):
                total = total + u_ref[STEP - 1 - k, vec(at - k * v), :]
            f_ref[vec(at), :] = total
        for at in range(start[1], depth, 8):
            g_ref[vec(at), :] = f_ref[vec(at), :] + pltpu.roll(
                f_ref[vec(at - STEP * v), :], 1, 1
            )
        for at in range(start[2], depth, 8):
            total = g_ref[vec(at), :] + pltpu.roll(
                g_ref[vec(at - 2 * STEP * v), :], 2, 1
            )
            s_refs[STEP - 1][vec(at), :] = total
            if at >= LEFT:
                into = vec(at - LEFT)
                b_ref[STEP - 1, into, :] = jnp.maximum(b_ref[STEP - 1, into, :], total)
        for t in range(STEP - 1):
            for at in range(start[3 + t], depth, 8):
                before = s_refs[t - 1][vec(at - v), :]
                if t == 0:
                    before = pltpu.roll(before, 1, 1)
                total = before + (u_ref[t, vec(at), :] - w_ref[t, vec(at - SEQ * v), :])
                if t < STEP - 2:
                    s_refs[t][vec(at), :] = total
                if at >= LEFT:
                    into = vec(at - LEFT)
                    b_ref[t, into, :] = jnp.maximum(b_ref[t, into, :], total)

    for tile in range(span // LANES):
        for t in range(STEP):
            count = (q_count - t + STEP - 1) // STEP
            turned = jnp.transpose(b_ref[t, pl.ds(tile * LANES, LANES), :])
            for h in range(2):
                o_ref[h * span // LANES + tile, pl.ds(t, count, stride=STEP), :] = turned[
                    h * HALF + AHEAD : h * HALF + AHEAD + count
                ]
    for tile in range(m_count // LANES):
        out_ref[0, :, pl.ds(tile * LANES, LANES)] = o_ref[tile]


def sequence_best(extended, slopes):
    rows, width = extended.shape
    m_count = width - LEFT - RIGHT
    tiles = (LEFT + m_count) // LANES
    span = m_count // 2
    depth = LEFT + span
    return pl.pallas_call(
        best_kernel,
        out_shape=jax.ShapeDtypeStruct((1, rows - LEAD, m_count), jnp.float32),
        in_specs=[
            pl.BlockSpec(memory_space=pltpu.SMEM),
            pl.BlockSpec(memory_space=pltpu.VMEM),
        ],
        out_specs=pl.BlockSpec(memory_space=pltpu.VMEM),
        scratch_shapes=[
            pltpu.VMEM((tiles, STEP * HALF, LANES), jnp.float32),
            pltpu.VMEM((STEP, depth, LANES), jnp.float32),
            pltpu.VMEM((STEP - 1, depth, LANES), jnp.float32),
            pltpu.VMEM((STEP, span, LANES), jnp.float32),
            pltpu.VMEM((m_count // LANES, rows - LEAD, LANES), jnp.float32),
        ]
        + [pltpu.VMEM((depth, LANES), jnp.float32)] * (STEP + 2),
        compiler_params=pltpu.CompilerParams(vmem_limit_bytes=40 << 20),
        name="best",
    )(slopes, extended)


def solution(mesh):
    npb, nma = mesh.shape["pb"], mesh.shape["ma"]

    def local(queries, map_descriptors, slopes):
        return sequence_best(score_tile(queries, map_descriptors, npb, nma), slopes)

    return jax.shard_map(
        local,
        mesh=mesh,
        in_specs=(P(None, ("pb", "ma"), None), P("ma", "pb"), P()),
        out_specs=P(None, "pb", "ma"),
        check_vma=False,
    )
```

```python
import math

import jax
import jax.numpy as jnp
from jax import lax
from jax.experimental import pallas as pl
from jax.experimental.pallas import tpu as pltpu
from jax.sharding import PartitionSpec as P

MESH = pl.DeviceIdType.MESH
SEQ = 20
RAD = 10
LEAD = 32
LEFT = 384
RIGHT = 128
LANES = 128
CORES = 2
STEP = 5
AHEAD = 8
HALF = 64
LAG = 2


def remote(src, dst, send, recv, where):
    return pltpu.make_async_remote_copy(
        src_ref=src,
        dst_ref=dst,
        send_sem=send,
        recv_sem=recv,
        device_id=where,
        device_id_type=MESH,
    )


def coded(block, narrow=True):
    top = jnp.max(jnp.abs(block), axis=1, keepdims=True)
    power = jnp.ceil(jnp.log2(jnp.maximum(top, 1e-30)) + 1e-3)
    code = jnp.floor(block * jnp.exp2(15.0 - power) + 0.5)
    code = jnp.clip(code, -32767.0, 32767.0)
    tail = jnp.broadcast_to(power, (block.shape[0], LANES))
    code, tail = code.astype(jnp.int32), tail.astype(jnp.int32)
    return (code.astype(jnp.int16), tail.astype(jnp.int16)) if narrow else (code, tail)


def band_of(depth, width, lead):
    inner = lax.broadcasted_iota(jnp.int32, (depth, width), 0)
    outer = lax.broadcasted_iota(jnp.int32, (depth, width), 1)
    near = jnp.abs(inner - lead - outer) <= RAD
    return jnp.where(near, 1.0, 0.0).astype(jnp.bfloat16)


def window(value, band):
    total = None
    for _ in range(2):
        part = value.astype(jnp.bfloat16)
        value = value - part.astype(jnp.float32)
        term = jnp.dot(part, band, preferred_element_type=jnp.float32)
        total = term if total is None else total + term
    return total * (1.0 / (2 * RAD + 1))


def whole(code):
    return code.astype(jnp.int32).astype(jnp.float32)


def score_kernel(
    npb,
    nma,
    q_ref,
    m_ref,
    c_ref,
    out_ref,
    q_all,
    m_all,
    p_out,
    p_in,
    r_out,
    l_out,
    l_in,
    r_in,
    local_sem,
    m_send,
    m_recv,
    y_send,
    y_recv,
    z_send,
    z_recv,
    x_send,
    x_recv,
    p_send,
    p_recv,
    halo_send,
    halo_recv,
    lead_send,
    lead_recv,
):
    pb, ma = lax.axis_index("pb"), lax.axis_index("ma")
    pair, across = npb // CORES, nma // 2
    row, core = pb // CORES, pb % CORES
    z, x = ma // 2, ma % 2
    each = q_all.shape[2]
    share = q_all.shape[3]
    m_count, half = m_ref.shape
    size = 2 * each
    last = across - 1
    mate = {"pb": row * CORES + 1 - core}
    twin = {"ma": z * 2 + 1 - x}
    block_of = [lax.rem(row + pair - k, pair) for k in range(pair)]
    row_at = [{"pb": lax.rem(row + k, pair) * CORES + core} for k in range(pair)]
    below, above = {"ma": ma - 2}, {"ma": ma + 2}
    has_below, has_above = z > 0, z < last
    has_up, has_down = pb > 0, pb < npb - 1
    offset = STEP * AHEAD - LEAD
    tiles = c_ref.shape[0]
    has_left, has_right = ma > 0, ma < nma - 1

    barrier = pltpu.get_barrier_semaphore()

    def greet(where):
        pl.semaphore_signal(barrier, inc=1, device_id=where, device_id_type=MESH)

    greet(mate)
    greet(twin)
    for k in range(1, pair):
        greet(row_at[k])
    sides = (
        (has_above, above),
        (has_below, below),
        (has_left, {"ma": ma - 1}),
        (has_right, {"ma": ma + 1}),
        (has_up, {"pb": pb - 1}),
        (has_down, {"pb": pb + 1}),
        (has_up & has_left, {"pb": pb - 1, "ma": ma - 1}),
        (has_up & has_right, {"pb": pb - 1, "ma": ma + 1}),
        (has_down & has_left, {"pb": pb + 1, "ma": ma - 1}),
        (has_down & has_right, {"pb": pb + 1, "ma": ma + 1}),
    )
    for test, where in sides:

        @pl.when(test)
        def _():
            greet(where)

    extra = sum(jnp.where(test, 1, 0) for test, _ in sides)
    pl.semaphore_wait(barrier, pair + 1 + extra)

    def part(k):
        at = pl.multiple_of(lax.rem(row + k, pair) * share, LANES)
        return q_ref.at[0, :, pl.ds(at, share)]

    to_row = [None] + [
        remote(part(k), q_all.at[row, ma], y_send.at[k], y_recv.at[k], row_at[k])
        for k in range(1, pair)
    ]
    for copy in to_row[1:]:
        copy.start()
    load_q = pltpu.make_async_copy(part(0), q_all.at[row, ma], local_sem.at[0])
    load_q.start()
    to_mate = remote(m_ref, m_all.at[core], m_send.at[0], m_recv.at[0], mate)
    to_mate.start()
    load_m = pltpu.make_async_copy(m_ref, m_all.at[core], local_sem.at[1])
    load_m.start()

    def ranked(e):
        far = lax.div(e + 1, 2)
        there = z + jnp.where(lax.rem(e, 2) == 1, -far, far)
        return there, (there >= 0) & (there <= last)

    def block_at(k, there, column):
        return q_all.at[block_of[k], there * 2 + column]

    def along_z(k, there, number, where):
        block = block_at(k, there, x)
        return remote(block, block, z_send.at[k, number], z_recv.at[k, there], where)

    def along_x(k, there):
        block = block_at(k, there, x)
        return remote(block, block, x_send.at[k, there], x_recv.at[k, there], twin)

    def spread(k):
        along_x(k, z).start()

        @pl.when(has_above)
        def _():
            along_z(k, z, z, above).start()

        @pl.when(has_below)
        def _():
            along_z(k, z, across, below).start()

    def forward(k, e):
        there, known = ranked(e)

        @pl.when(known)
        def _():
            along_z(k, there, there, twin).wait_recv()
            along_x(k, there).start()

        @pl.when(known & (there < z) & has_above)
        def _():
            along_z(k, there, there, above).start()

        @pl.when(known & (there > z) & has_below)
        def _():
            along_z(k, there, there, below).start()

    def from_x(k, there):
        block = block_at(k, there, 1 - x)
        return remote(block, block, x_send.at[k, there], x_recv.at[k, there], twin)

    load_q.wait()
    spread(0)
    forward(0, 1)
    forward(0, 2)
    for k in range(1, pair):
        to_row[k].wait_recv()
        spread(k)

    load_m.wait()
    to_mate.wait_recv()

    @pl.when(pb == 0)
    def _():
        c_ref[:, pl.ds(offset, LEAD), :] = jnp.zeros((tiles, LEAD, LANES), jnp.float32)

    @pl.when(ma == 0)
    def _():
        out_ref[:, pl.ds(0, LEFT)] = jnp.zeros((out_ref.shape[0], LEFT), jnp.float32)

    @pl.when(ma == nma - 1)
    def _():
        out_ref[:, pl.ds(LEFT + m_count, RIGHT)] = jnp.zeros(
            (out_ref.shape[0], RIGHT), jnp.float32
        )

    def score(k, there):
        block = q_all[block_of[k], pl.ds(there * 2, 2)]
        if each % 16 == 0:
            block = block.reshape(size, share)
        else:
            block = block.astype(jnp.float32).reshape(size, share).astype(block.dtype)
        total = None
        for slot in range(CORES):
            term = lax.dot_general(
                block[:, slot * half : (slot + 1) * half],
                m_all[slot],
                (((1,), (1,)), ((), ())),
                preferred_element_type=jnp.float32,
            )
            total = term if total is None else total + term
        return total

    def partial(k, there):
        return remote(
            p_out.at[k - 1, there],
            p_in.at[k - 1, there],
            p_send.at[k - 1, there],
            p_recv.at[k - 1, there],
            row_at[pair - k],
        )

    def add_partials(e):
        there, known = ranked(e)
        for k in range(1, pair):

            @pl.when(known)
            def _():
                from_x(k, there).wait_recv()
                code, tail = coded(score(k, there))
                p_out[k - 1, there, :, pl.ds(0, m_count)] = code
                p_out[k - 1, there, :, pl.ds(m_count, LANES)] = tail
                partial(k, there).start()

    lead_each = min(LEAD, size)
    lead_parts = LEAD // lead_each

    def halos(there):
        right = remote(
            r_out.at[there], l_in.at[there], halo_send.at[0, there], halo_recv.at[0, there],
            {"ma": ma + 1},
        )
        left = remote(
            l_out.at[there], r_in.at[there], halo_send.at[1, there], halo_recv.at[1, there],
            {"ma": ma - 1},
        )
        return (has_right, has_left, right), (has_left, has_right, left)

    def leads(number):
        there = across - lead_parts + number
        rows = pl.ds(size - lead_each, lead_each)
        into = pl.ds(number * lead_each, lead_each)
        slot = across + number
        down, up = has_down, has_up
        main = remote(
            out_ref.at[pl.ds(LEAD + (there + 1) * size - lead_each, lead_each), pl.ds(LEFT, m_count)],
            out_ref.at[into, pl.ds(LEFT, m_count)],
            lead_send.at[0, number], lead_recv.at[0, number], {"pb": pb + 1},
        )
        right = remote(
            r_out.at[there, rows], l_in.at[slot, pl.ds(0, lead_each)],
            lead_send.at[1, number], lead_recv.at[1, number], {"pb": pb + 1, "ma": ma + 1},
        )
        left = remote(
            l_out.at[there, rows], r_in.at[slot, pl.ds(0, lead_each)],
            lead_send.at[2, number], lead_recv.at[2, number], {"pb": pb + 1, "ma": ma - 1},
        )
        return (
            (down, up, main),
            (down & has_right, up & has_left, right),
            (down & has_left, up & has_right, left),
        )

    def start(group):
        for sends, _, copy in group:

            @pl.when(sends)
            def _():
                copy.start()

    def edged(block, spare):
        code, tail = coded(block, narrow=False)
        lane = lax.broadcasted_iota(jnp.int32, code.shape, 1)
        if code.shape[1] > LANES:
            tail = jnp.concatenate([tail] * (code.shape[1] // LANES), axis=1)
        return jnp.where((lane >= spare) & (lane < spare + 16), tail, code).astype(jnp.int16)

    def opened(code, spare):
        value = whole(code)
        return value * jnp.exp2(value[:, spare : spare + 1] - 15.0)

    edge = band_of(2 * LANES, LANES, 0)
    inside = band_of(4 * LANES, 2 * LANES, LANES)

    def contrast(at, count, tile, lead, band):
        value = out_ref[pl.ds(at, count), pl.ds(tile * LANES - lead, band.shape[0])]
        width = band.shape[1]
        centre = value[:, lead : lead + width]
        average = window(value, band)
        spread = window(value * value, band) - average * average
        normal = (centre - average) * (
            lax.rsqrt(spread + 1.0) * (1.0 / math.sqrt(SEQ))
        )
        for side in range(width // LANES):
            part = normal[:, side * LANES : (side + 1) * LANES]
            if tile + side < LEFT // LANES:
                part = jnp.where(ma == 0, 0.0, part)
            c_ref[tile + side, pl.ds(at + offset, count), :] = part

    inner_tiles = range(LEFT // LANES + 2, tiles - 2, 2)
    outer_tiles = [t for t in range(1, tiles, 2) if t not in inner_tiles]

    def outer(at, count):
        contrast(at, count, 0, 0, edge)
        for tile in outer_tiles:
            contrast(at, count, tile, LANES, inside)

    def own(e):
        there, known = ranked(e)

        @pl.when(known)
        def _():
            from_x(0, there).wait_recv()
            total = score(0, there)
            for k in range(1, pair):
                partial(k, there).wait_recv()
                scale = jnp.exp2(whole(p_in[k - 1, there, :, pl.ds(m_count, LANES)]) - 15.0)
                code = whole(p_in[k - 1, there, :, pl.ds(0, m_count)])
                total = total + code * scale[:, :1]
            at = pl.multiple_of(LEAD + there * size, 8)
            out_ref[pl.ds(at, size), pl.ds(LEFT, m_count)] = total
            for tile in inner_tiles:
                contrast(at, size, tile, LANES, inside)
            r_out[there] = edged(total[:, m_count - LEFT :], 0)
            l_out[there] = edged(total[:, :RIGHT], LANES - 16)
            start(halos(there))
            for number in range(lead_parts):

                @pl.when(there == across - lead_parts + number)
                def _():
                    start(leads(number))

    def finish(group):
        for sends, receives, copy in group:

            @pl.when(receives)
            def _():
                copy.wait_recv()

            @pl.when(sends)
            def _():
                copy.wait_send()

    def unpack(rows, slot, count):
        @pl.when(has_left)
        def _():
            out_ref[rows, pl.ds(0, LEFT)] = opened(l_in[slot, pl.ds(0, count)], 0)

        @pl.when(has_right)
        def _():
            out_ref[rows, pl.ds(LEFT + m_count, RIGHT)] = opened(
                r_in[slot, pl.ds(0, count)], LANES - 16
            )

    def outline(e):
        there, known = ranked(e)

        @pl.when(known)
        def _():
            finish(halos(there))
            at = pl.multiple_of(LEAD + there * size, 8)
            unpack(pl.ds(at, size), there, size)
            outer(at, size)

    def at_distance(d, act):
        @pl.when(d >= 0)
        def _():
            @pl.when(d > 0)
            def _():
                act(2 * d - 1)

            act(2 * d)

    @pl.loop(0, across + 2 * LAG)
    def _(d):
        for e in (2 * d + 1, 2 * d + 2):
            for k in range(1, pair):
                forward(k, e)

        @pl.when(d > 1)
        def _():
            for e in (2 * d - 1, 2 * d):
                forward(0, e)

        at_distance(d, add_partials)
        at_distance(d - LAG, own)
        at_distance(d - 2 * LAG, outline)

    @pl.loop(0, 2 * across - 1)
    def _(e):
        there, known = ranked(e)

        @pl.when(known)
        def _():
            for k in range(1, pair):
                partial(k, there).wait_send()
            for k in range(pair):
                along_x(k, there).wait_send()

        onward = ((there < z) & has_above) | ((there > z) & has_below)
        for k in range(pair):

            @pl.when(known & onward)
            def _():
                along_z(k, there, there, twin).wait_send()

    for number in range(lead_parts):
        finish(leads(number))

        @pl.when(has_up)
        def _():
            unpack(pl.ds(number * lead_each, lead_each), across + number, lead_each)
            for tile in inner_tiles:
                contrast(number * lead_each, lead_each, tile, LANES, inside)
            outer(number * lead_each, lead_each)

    for k in range(1, pair):
        to_row[k].wait_send()
    to_mate.wait_send()
    for k in range(pair):

        @pl.when(has_above)
        def _():
            along_z(k, z, z, above).wait_send()

        @pl.when(has_below)
        def _():
            along_z(k, z, across, below).wait_send()


def score_tile(queries, map_descriptors, npb, nma):
    each, width = queries.shape[1:]
    m_count, half = map_descriptors.shape
    q_count = each * nma
    pair, across = npb // CORES, nma // 2
    size = 2 * each
    parts = LEAD // min(LEAD, size)
    dma = pltpu.SemaphoreType.DMA
    return pl.pallas_call(
        lambda *refs: score_kernel(npb, nma, *refs),
        out_shape=jax.ShapeDtypeStruct(
            ((LEFT + m_count) // LANES, STEP * HALF, LANES), jnp.float32
        ),
        in_specs=[pl.BlockSpec(memory_space=pltpu.HBM)] * 2,
        out_specs=pl.BlockSpec(memory_space=pltpu.VMEM),
        scratch_shapes=[
            pltpu.VMEM((LEAD + q_count, LEFT + m_count + RIGHT), jnp.float32),
            pltpu.VMEM((pair, nma, each, width // pair), jnp.bfloat16),
            pltpu.VMEM((CORES, m_count, half), jnp.bfloat16),
            pltpu.VMEM((pair - 1, across, size, m_count + LANES), jnp.int16),
            pltpu.VMEM((pair - 1, across, size, m_count + LANES), jnp.int16),
            pltpu.VMEM((across, size, LEFT), jnp.int16),
            pltpu.VMEM((across, size, RIGHT), jnp.int16),
            pltpu.VMEM((across + parts, size, LEFT), jnp.int16),
            pltpu.VMEM((across + parts, size, RIGHT), jnp.int16),
            dma((2,)),
            dma((1,)),
            dma((1,)),
            dma((pair,)),
            dma((pair,)),
            dma((pair, across + 1)),
            dma((pair, across)),
            dma((pair, across)),
            dma((pair, across)),
            dma((pair - 1, across)),
            dma((pair - 1, across)),
            dma((2, across)),
            dma((2, across)),
            dma((3, across)),
            dma((3, across)),
        ],
        compiler_params=pltpu.CompilerParams(
            collective_id=0, has_side_effects=True, vmem_limit_bytes=32 << 20
        ),
        name="scores",
    )(queries, map_descriptors)


def best_kernel(slopes_ref, c_ref, out_ref, u_ref, w_ref, b_ref, o_ref, *scratch):
    q_count, m_count = out_ref.shape[1:]

    span = m_count // 2
    depth = LEFT + span
    for t in range(STEP):
        for tile in range(depth // LANES):
            both = [
                c_ref[h * span // LANES + tile, pl.ds(t, HALF, stride=STEP), :]
                for h in range(2)
            ]
            turned = jnp.transpose(jnp.concatenate(both, axis=0))
            at = pl.ds(tile * LANES, LANES)
            u_ref[t, at, :] = turned
            if t < STEP - 1:
                w_ref[t, at, :] = pltpu.roll(turned, SEQ // STEP, 1)

    b_ref[...] = jnp.full(b_ref.shape, -jnp.inf, jnp.float32)
    start = LEFT - 288, LEFT - 216, LEFT - 64, LEFT - 48, LEFT - 32, LEFT - 16, LEFT

    def vec(at):
        return pl.ds(at, 8)

    joint = len(scratch) // (STEP + 1)
    stages = [scratch[n * (STEP + 1) : (n + 1) * (STEP + 1)] for n in range(joint)]

    @pl.loop(0, slopes_ref.shape[0] // joint)
    def _(index):
        known = [(slopes_ref[index * joint + n], *stages[n]) for n in range(joint)]
        for at in range(start[0], depth, 8):
            here = u_ref[STEP - 1, vec(at), :]
            for v, f_ref, *_ in known:
                total = here
                for k in range(1, STEP):
                    total = total + u_ref[STEP - 1 - k, vec(at - k * v), :]
                f_ref[vec(at), :] = total
        for at in range(start[1], depth, 8):
            for v, f_ref, g_ref, *_ in known:
                g_ref[vec(at), :] = f_ref[vec(at), :] + pltpu.roll(
                    f_ref[vec(at - STEP * v), :], 1, 1
                )
        for at in range(start[2], depth, 8):
            into = vec(at - LEFT)
            best = b_ref[STEP - 1, into, :] if at >= LEFT else None
            for v, _, g_ref, s_ref, *_ in known:
                total = g_ref[vec(at), :] + pltpu.roll(
                    g_ref[vec(at - 2 * STEP * v), :], 2, 1
                )
                s_ref[vec(at), :] = total
                best = None if best is None else jnp.maximum(best, total)
            if best is not None:
                b_ref[STEP - 1, into, :] = best
        for t in range(STEP - 1):
            for at in range(start[3 + t], depth, 8):
                into = vec(at - LEFT)
                best = b_ref[t, into, :] if at >= LEFT else None
                here = u_ref[t, vec(at), :]
                for v, _, _, *s_refs in known:
                    before = s_refs[t][vec(at - v), :]
                    if t == 0:
                        before = pltpu.roll(before, 1, 1)
                    total = before + (here - w_ref[t, vec(at - SEQ * v), :])
                    if t < STEP - 2:
                        s_refs[t + 1][vec(at), :] = total
                    best = None if best is None else jnp.maximum(best, total)
                if best is not None:
                    b_ref[t, into, :] = best

    for tile in range(span // LANES):
        for t in range(STEP):
            count = (q_count - t + STEP - 1) // STEP
            turned = jnp.transpose(b_ref[t, pl.ds(tile * LANES, LANES), :])
            for h in range(2):
                o_ref[h * span // LANES + tile, pl.ds(t, count, stride=STEP), :] = turned[
                    h * HALF + AHEAD : h * HALF + AHEAD + count
                ]
    for tile in range(m_count // LANES):
        out_ref[0, :, pl.ds(tile * LANES, LANES)] = o_ref[tile]


JOINT = 4


def sequence_best(contrasts, slopes, q_count, m_count):
    span = m_count // 2
    depth = LEFT + span
    joint = math.gcd(JOINT, slopes.shape[0])
    return pl.pallas_call(
        best_kernel,
        out_shape=jax.ShapeDtypeStruct((1, q_count, m_count), jnp.float32),
        in_specs=[
            pl.BlockSpec(memory_space=pltpu.SMEM),
            pl.BlockSpec(memory_space=pltpu.VMEM),
        ],
        out_specs=pl.BlockSpec(memory_space=pltpu.VMEM),
        scratch_shapes=[
            pltpu.VMEM((STEP, depth, LANES), jnp.float32),
            pltpu.VMEM((STEP - 1, depth, LANES), jnp.float32),
            pltpu.VMEM((STEP, span, LANES), jnp.float32),
            pltpu.VMEM((m_count // LANES, q_count, LANES), jnp.float32),
        ]
        + [pltpu.VMEM((depth, LANES), jnp.float32)] * (joint * (STEP + 1)),
        compiler_params=pltpu.CompilerParams(vmem_limit_bytes=40 << 20),
        name="best",
    )(slopes, contrasts)


def solution(mesh):
    npb, nma = mesh.shape["pb"], mesh.shape["ma"]

    def local(queries, map_descriptors, slopes):
        q_count, m_count = queries.shape[1] * nma, map_descriptors.shape[0]
        queries = pltpu.with_memory_space_constraint(queries, pltpu.HBM)
        map_descriptors = pltpu.with_memory_space_constraint(map_descriptors, pltpu.HBM)
        contrasts = score_tile(queries, map_descriptors, npb, nma)
        return sequence_best(contrasts, slopes, q_count, m_count)

    return jax.shard_map(
        local,
        mesh=mesh,
        in_specs=(P(None, ("pb", "ma"), None), P("ma", "pb"), P()),
        out_specs=P(None, "pb", "ma"),
        check_vma=False,
    )
```

```python
import math

import jax
import jax.numpy as jnp
from jax import lax
from jax.experimental import pallas as pl
from jax.experimental.pallas import tpu as pltpu
from jax.sharding import PartitionSpec as P

MESH = pl.DeviceIdType.MESH
SEQ = 20
RAD = 10
LEAD = 32
LEFT = 384
RIGHT = 128
LANES = 128
CORES = 2
STEP = 5
AHEAD = 8
HALF = 64
LAG = 3


def remote(src, dst, send, recv, where):
    return pltpu.make_async_remote_copy(
        src_ref=src,
        dst_ref=dst,
        send_sem=send,
        recv_sem=recv,
        device_id=where,
        device_id_type=MESH,
    )


def coded(block, narrow=True):
    top = jnp.max(jnp.abs(block), axis=1, keepdims=True)
    power = jnp.ceil(jnp.log2(jnp.maximum(top, 1e-30)) + 1e-3)
    code = jnp.floor(block * jnp.exp2(15.0 - power) + 0.5)
    code = jnp.clip(code, -32767.0, 32767.0)
    tail = jnp.broadcast_to(power, (block.shape[0], LANES))
    code, tail = code.astype(jnp.int32), tail.astype(jnp.int32)
    return (code.astype(jnp.int16), tail.astype(jnp.int16)) if narrow else (code, tail)


def band_of(depth, width, lead):
    inner = lax.broadcasted_iota(jnp.int32, (depth, width), 0)
    outer = lax.broadcasted_iota(jnp.int32, (depth, width), 1)
    near = jnp.abs(inner - lead - outer) <= RAD
    return jnp.where(near, 1.0, 0.0).astype(jnp.bfloat16)


def windows(value, band):
    terms = []
    for item in (value, value * value):
        high = item.astype(jnp.bfloat16)
        terms += [high, (item - high.astype(jnp.float32)).astype(jnp.bfloat16)]
    total = jnp.dot(
        jnp.concatenate(terms, axis=0), band, preferred_element_type=jnp.float32
    )
    rows = value.shape[0]
    part = [total[n * rows : (n + 1) * rows] for n in range(4)]
    scale = 1.0 / (2 * RAD + 1)
    return (part[0] + part[1]) * scale, (part[2] + part[3]) * scale


def whole(code):
    return code.astype(jnp.int32).astype(jnp.float32)


def score_kernel(
    npb,
    nma,
    q_ref,
    m_ref,
    c_ref,
    out_ref,
    q_all,
    m_all,
    p_out,
    p_in,
    r_out,
    l_out,
    l_in,
    r_in,
    local_sem,
    m_send,
    m_recv,
    y_send,
    y_recv,
    z_send,
    z_recv,
    x_send,
    x_recv,
    p_send,
    p_recv,
    halo_send,
    halo_recv,
    lead_send,
    lead_recv,
):
    pb, ma = lax.axis_index("pb"), lax.axis_index("ma")
    pair, across = npb // CORES, nma // 2
    row, core = pb // CORES, pb % CORES
    z, x = ma // 2, ma % 2
    each = q_all.shape[2]
    share = q_all.shape[3]
    m_count, half = m_ref.shape
    size = 2 * each
    last = across - 1
    mate = {"pb": row * CORES + 1 - core}
    twin = {"ma": z * 2 + 1 - x}
    block_of = [lax.rem(row + pair - k, pair) for k in range(pair)]
    row_at = [{"pb": lax.rem(row + k, pair) * CORES + core} for k in range(pair)]
    below, above = {"ma": ma - 2}, {"ma": ma + 2}
    has_below, has_above = z > 0, z < last
    has_up, has_down = pb > 0, pb < npb - 1
    offset = STEP * AHEAD - LEAD
    tiles = c_ref.shape[0]
    has_left, has_right = ma > 0, ma < nma - 1

    barrier = pltpu.get_barrier_semaphore()

    def greet(where):
        pl.semaphore_signal(barrier, inc=1, device_id=where, device_id_type=MESH)

    greet(mate)
    greet(twin)
    for k in range(1, pair):
        greet(row_at[k])
    sides = (
        (has_above, above),
        (has_below, below),
        (has_left, {"ma": ma - 1}),
        (has_right, {"ma": ma + 1}),
        (has_up, {"pb": pb - 1}),
        (has_down, {"pb": pb + 1}),
        (has_up & has_left, {"pb": pb - 1, "ma": ma - 1}),
        (has_up & has_right, {"pb": pb - 1, "ma": ma + 1}),
        (has_down & has_left, {"pb": pb + 1, "ma": ma - 1}),
        (has_down & has_right, {"pb": pb + 1, "ma": ma + 1}),
    )
    for test, where in sides:

        @pl.when(test)
        def _():
            greet(where)

    extra = sum(jnp.where(test, 1, 0) for test, _ in sides)
    pl.semaphore_wait(barrier, pair + 1 + extra)

    def part(k):
        at = pl.multiple_of(lax.rem(row + k, pair) * share, LANES)
        return q_ref.at[0, :, pl.ds(at, share)]

    to_row = [None] + [
        remote(part(k), q_all.at[row, ma], y_send.at[k], y_recv.at[k], row_at[k])
        for k in range(1, pair)
    ]
    for copy in to_row[1:]:
        copy.start()
    load_q = pltpu.make_async_copy(part(0), q_all.at[row, ma], local_sem.at[0])
    load_q.start()
    to_mate = remote(m_ref, m_all.at[core], m_send.at[0], m_recv.at[0], mate)
    to_mate.start()
    load_m = pltpu.make_async_copy(m_ref, m_all.at[core], local_sem.at[1])
    load_m.start()

    def ranked(e):
        far = lax.div(e + 1, 2)
        there = z + jnp.where(lax.rem(e, 2) == 1, -far, far)
        return there, (there >= 0) & (there <= last)

    def block_at(k, there, column):
        return q_all.at[block_of[k], there * 2 + column]

    def along_z(k, there, number, where):
        block = block_at(k, there, x)
        return remote(block, block, z_send.at[k, number], z_recv.at[k, there], where)

    def along_x(k, there):
        block = block_at(k, there, x)
        return remote(block, block, x_send.at[k, there], x_recv.at[k, there], twin)

    def spread(k):
        along_x(k, z).start()

        @pl.when(has_above)
        def _():
            along_z(k, z, z, above).start()

        @pl.when(has_below)
        def _():
            along_z(k, z, across, below).start()

    def forward(k, e):
        there, known = ranked(e)

        @pl.when(known)
        def _():
            along_z(k, there, there, twin).wait_recv()
            along_x(k, there).start()

        @pl.when(known & (there < z) & has_above)
        def _():
            along_z(k, there, there, above).start()

        @pl.when(known & (there > z) & has_below)
        def _():
            along_z(k, there, there, below).start()

    def from_x(k, there):
        block = block_at(k, there, 1 - x)
        return remote(block, block, x_send.at[k, there], x_recv.at[k, there], twin)

    load_q.wait()
    spread(0)
    forward(0, 1)
    forward(0, 2)
    for k in range(1, pair):
        to_row[k].wait_recv()
        spread(k)

    load_m.wait()
    to_mate.wait_recv()

    @pl.when(pb == 0)
    def _():
        c_ref[:, pl.ds(offset, LEAD), :] = jnp.zeros((tiles, LEAD, LANES), jnp.float32)

    @pl.when(ma == 0)
    def _():
        out_ref[:, pl.ds(0, LEFT)] = jnp.zeros((out_ref.shape[0], LEFT), jnp.float32)

    @pl.when(ma == nma - 1)
    def _():
        out_ref[:, pl.ds(LEFT + m_count, RIGHT)] = jnp.zeros(
            (out_ref.shape[0], RIGHT), jnp.float32
        )

    def score(k, there):
        block = q_all[block_of[k], pl.ds(there * 2, 2)]
        if each % 16 == 0:
            block = block.reshape(size, share)
        else:
            block = block.astype(jnp.float32).reshape(size, share).astype(block.dtype)
        total = None
        for slot in range(CORES):
            term = lax.dot_general(
                block[:, slot * half : (slot + 1) * half],
                m_all[slot],
                (((1,), (1,)), ((), ())),
                preferred_element_type=jnp.float32,
            )
            total = term if total is None else total + term
        return total

    def partial(k, there):
        return remote(
            p_out.at[k - 1, there],
            p_in.at[k - 1, there],
            p_send.at[k - 1, there],
            p_recv.at[k - 1, there],
            row_at[pair - k],
        )

    def add_partials(e):
        there, known = ranked(e)
        for k in range(1, pair):

            @pl.when(known)
            def _():
                from_x(k, there).wait_recv()
                code, tail = coded(score(k, there))
                p_out[k - 1, there, :, pl.ds(0, m_count)] = code
                p_out[k - 1, there, :, pl.ds(m_count, LANES)] = tail
                partial(k, there).start()

    lead_each = min(LEAD, size)
    lead_parts = LEAD // lead_each

    def halos(there):
        right = remote(
            r_out.at[there], l_in.at[there], halo_send.at[0, there], halo_recv.at[0, there],
            {"ma": ma + 1},
        )
        left = remote(
            l_out.at[there], r_in.at[there], halo_send.at[1, there], halo_recv.at[1, there],
            {"ma": ma - 1},
        )
        return (has_right, has_left, right), (has_left, has_right, left)

    def leads(number):
        there = across - lead_parts + number
        rows = pl.ds(size - lead_each, lead_each)
        into = pl.ds(number * lead_each, lead_each)
        slot = across + number
        down, up = has_down, has_up
        main = remote(
            out_ref.at[pl.ds(LEAD + (there + 1) * size - lead_each, lead_each), pl.ds(LEFT, m_count)],
            out_ref.at[into, pl.ds(LEFT, m_count)],
            lead_send.at[0, number], lead_recv.at[0, number], {"pb": pb + 1},
        )
        right = remote(
            r_out.at[there, rows], l_in.at[slot, pl.ds(0, lead_each)],
            lead_send.at[1, number], lead_recv.at[1, number], {"pb": pb + 1, "ma": ma + 1},
        )
        left = remote(
            l_out.at[there, rows], r_in.at[slot, pl.ds(0, lead_each)],
            lead_send.at[2, number], lead_recv.at[2, number], {"pb": pb + 1, "ma": ma - 1},
        )
        return (
            (down, up, main),
            (down & has_right, up & has_left, right),
            (down & has_left, up & has_right, left),
        )

    def start(group):
        for sends, _, copy in group:

            @pl.when(sends)
            def _():
                copy.start()

    def edged(block, spare):
        code, tail = coded(block, narrow=False)
        lane = lax.broadcasted_iota(jnp.int32, code.shape, 1)
        if code.shape[1] > LANES:
            tail = jnp.concatenate([tail] * (code.shape[1] // LANES), axis=1)
        return jnp.where((lane >= spare) & (lane < spare + 16), tail, code).astype(jnp.int16)

    def opened(code, spare):
        value = whole(code)
        return value * jnp.exp2(value[:, spare : spare + 1] - 15.0)

    edge = band_of(2 * LANES, LANES, 0)
    inside = band_of(4 * LANES, 2 * LANES, LANES)

    def contrast(at, count, tile, lead, band):
        value = out_ref[pl.ds(at, count), pl.ds(tile * LANES - lead, band.shape[0])]
        width = band.shape[1]
        centre = value[:, lead : lead + width]
        average, square = windows(value, band)
        spread = square - average * average
        normal = (centre - average) * (
            lax.rsqrt(spread + 1.0) * (1.0 / math.sqrt(SEQ))
        )
        for side in range(width // LANES):
            part = normal[:, side * LANES : (side + 1) * LANES]
            if tile + side < LEFT // LANES:
                part = jnp.where(ma == 0, 0.0, part)
            c_ref[tile + side, pl.ds(at + offset, count), :] = part

    inner_tiles = range(LEFT // LANES + 2, tiles - 2, 2)
    outer_tiles = [t for t in range(1, tiles, 2) if t not in inner_tiles]

    def outer(at, count):
        contrast(at, count, 0, 0, edge)
        for tile in outer_tiles:
            contrast(at, count, tile, LANES, inside)

    def own(e):
        there, known = ranked(e)

        @pl.when(known)
        def _():
            from_x(0, there).wait_recv()
            total = score(0, there)
            for k in range(1, pair):
                partial(k, there).wait_recv()
                scale = jnp.exp2(whole(p_in[k - 1, there, :, pl.ds(m_count, LANES)]) - 15.0)
                code = whole(p_in[k - 1, there, :, pl.ds(0, m_count)])
                total = total + code * scale[:, :1]
            at = pl.multiple_of(LEAD + there * size, 8)
            out_ref[pl.ds(at, size), pl.ds(LEFT, m_count)] = total
            r_out[there] = edged(total[:, m_count - LEFT :], 0)
            l_out[there] = edged(total[:, :RIGHT], LANES - 16)
            start(halos(there))
            for number in range(lead_parts):

                @pl.when(there == across - lead_parts + number)
                def _():
                    start(leads(number))

            for tile in inner_tiles:
                contrast(at, size, tile, LANES, inside)

    def finish(group):
        for sends, receives, copy in group:

            @pl.when(receives)
            def _():
                copy.wait_recv()

            @pl.when(sends)
            def _():
                copy.wait_send()

    def unpack(rows, slot, count):
        @pl.when(has_left)
        def _():
            out_ref[rows, pl.ds(0, LEFT)] = opened(l_in[slot, pl.ds(0, count)], 0)

        @pl.when(has_right)
        def _():
            out_ref[rows, pl.ds(LEFT + m_count, RIGHT)] = opened(
                r_in[slot, pl.ds(0, count)], LANES - 16
            )

    def outline(e):
        there, known = ranked(e)

        @pl.when(known)
        def _():
            finish(halos(there))
            at = pl.multiple_of(LEAD + there * size, 8)
            unpack(pl.ds(at, size), there, size)
            outer(at, size)

    def at_distance(d, act):
        @pl.when(d >= 0)
        def _():
            @pl.when(d > 0)
            def _():
                act(2 * d - 1)

            act(2 * d)

    @pl.loop(0, across + 2 * LAG)
    def _(d):
        for e in (2 * d + 1, 2 * d + 2):
            for k in range(1, pair):
                forward(k, e)

        @pl.when(d > 1)
        def _():
            for e in (2 * d - 1, 2 * d):
                forward(0, e)

        at_distance(d, add_partials)
        at_distance(d - LAG, own)
        at_distance(d - 2 * LAG, outline)

    @pl.loop(0, 2 * across - 1)
    def _(e):
        there, known = ranked(e)

        @pl.when(known)
        def _():
            for k in range(1, pair):
                partial(k, there).wait_send()
            for k in range(pair):
                along_x(k, there).wait_send()

        onward = ((there < z) & has_above) | ((there > z) & has_below)
        for k in range(pair):

            @pl.when(known & onward)
            def _():
                along_z(k, there, there, twin).wait_send()

    for number in range(lead_parts):
        finish(leads(number))

        @pl.when(has_up)
        def _():
            unpack(pl.ds(number * lead_each, lead_each), across + number, lead_each)
            for tile in inner_tiles:
                contrast(number * lead_each, lead_each, tile, LANES, inside)
            outer(number * lead_each, lead_each)

    for k in range(1, pair):
        to_row[k].wait_send()
    to_mate.wait_send()
    for k in range(pair):

        @pl.when(has_above)
        def _():
            along_z(k, z, z, above).wait_send()

        @pl.when(has_below)
        def _():
            along_z(k, z, across, below).wait_send()


def score_tile(queries, map_descriptors, npb, nma):
    each, width = queries.shape[1:]
    m_count, half = map_descriptors.shape
    q_count = each * nma
    pair, across = npb // CORES, nma // 2
    size = 2 * each
    parts = LEAD // min(LEAD, size)
    dma = pltpu.SemaphoreType.DMA
    return pl.pallas_call(
        lambda *refs: score_kernel(npb, nma, *refs),
        out_shape=jax.ShapeDtypeStruct(
            ((LEFT + m_count) // LANES, STEP * HALF, LANES), jnp.float32
        ),
        in_specs=[pl.BlockSpec(memory_space=pltpu.HBM)] * 2,
        out_specs=pl.BlockSpec(memory_space=pltpu.VMEM),
        scratch_shapes=[
            pltpu.VMEM((LEAD + q_count, LEFT + m_count + RIGHT), jnp.float32),
            pltpu.VMEM((pair, nma, each, width // pair), jnp.bfloat16),
            pltpu.VMEM((CORES, m_count, half), jnp.bfloat16),
            pltpu.VMEM((pair - 1, across, size, m_count + LANES), jnp.int16),
            pltpu.VMEM((pair - 1, across, size, m_count + LANES), jnp.int16),
            pltpu.VMEM((across, size, LEFT), jnp.int16),
            pltpu.VMEM((across, size, RIGHT), jnp.int16),
            pltpu.VMEM((across + parts, size, LEFT), jnp.int16),
            pltpu.VMEM((across + parts, size, RIGHT), jnp.int16),
            dma((2,)),
            dma((1,)),
            dma((1,)),
            dma((pair,)),
            dma((pair,)),
            dma((pair, across + 1)),
            dma((pair, across)),
            dma((pair, across)),
            dma((pair, across)),
            dma((pair - 1, across)),
            dma((pair - 1, across)),
            dma((2, across)),
            dma((2, across)),
            dma((3, across)),
            dma((3, across)),
        ],
        compiler_params=pltpu.CompilerParams(
            collective_id=0, has_side_effects=True, vmem_limit_bytes=32 << 20
        ),
        name="scores",
    )(queries, map_descriptors)


def best_kernel(slopes_ref, c_ref, out_ref, u_ref, w_ref, b_ref, o_ref, *scratch):
    q_count, m_count = out_ref.shape[1:]

    span = m_count // 2
    depth = LEFT + span
    for t in range(STEP):
        for tile in range(depth // LANES):
            both = [
                c_ref[h * span // LANES + tile, pl.ds(t, HALF, stride=STEP), :]
                for h in range(2)
            ]
            turned = jnp.transpose(jnp.concatenate(both, axis=0))
            at = pl.ds(tile * LANES, LANES)
            u_ref[t, at, :] = turned
            if t < STEP - 1:
                w_ref[t, at, :] = pltpu.roll(turned, SEQ // STEP, 1)

    b_ref[...] = jnp.full(b_ref.shape, -jnp.inf, jnp.float32)
    start = LEFT - 288, LEFT - 216, LEFT - 64, LEFT - 48, LEFT - 32, LEFT - 16, LEFT

    def vec(at):
        return pl.ds(at, 8)

    joint = len(scratch) // (STEP + 1)
    stages = [scratch[n * (STEP + 1) : (n + 1) * (STEP + 1)] for n in range(joint)]

    @pl.loop(0, slopes_ref.shape[0] // joint)
    def _(index):
        known = [(slopes_ref[index * joint + n], *stages[n]) for n in range(joint)]
        for at in range(start[0], depth, 8):
            here = u_ref[STEP - 1, vec(at), :]
            for v, f_ref, *_ in known:
                total = here
                for k in range(1, STEP):
                    total = total + u_ref[STEP - 1 - k, vec(at - k * v), :]
                f_ref[vec(at), :] = total
        for at in range(start[1], depth, 8):
            for v, f_ref, g_ref, *_ in known:
                g_ref[vec(at), :] = f_ref[vec(at), :] + pltpu.roll(
                    f_ref[vec(at - STEP * v), :], 1, 1
                )
        for at in range(start[2], depth, 8):
            into = vec(at - LEFT)
            best = b_ref[STEP - 1, into, :] if at >= LEFT else None
            for v, _, g_ref, s_ref, *_ in known:
                total = g_ref[vec(at), :] + pltpu.roll(
                    g_ref[vec(at - 2 * STEP * v), :], 2, 1
                )
                s_ref[vec(at), :] = total
                best = None if best is None else jnp.maximum(best, total)
            if best is not None:
                b_ref[STEP - 1, into, :] = best
        for t in range(STEP - 1):
            for at in range(start[3 + t], depth, 8):
                into = vec(at - LEFT)
                best = b_ref[t, into, :] if at >= LEFT else None
                here = u_ref[t, vec(at), :]
                for v, _, _, *s_refs in known:
                    before = s_refs[t][vec(at - v), :]
                    if t == 0:
                        before = pltpu.roll(before, 1, 1)
                    total = before + (here - w_ref[t, vec(at - SEQ * v), :])
                    if t < STEP - 2:
                        s_refs[t + 1][vec(at), :] = total
                    best = None if best is None else jnp.maximum(best, total)
                if best is not None:
                    b_ref[t, into, :] = best

    for tile in range(span // LANES):
        for t in range(STEP):
            count = (q_count - t + STEP - 1) // STEP
            turned = jnp.transpose(b_ref[t, pl.ds(tile * LANES, LANES), :])
            for h in range(2):
                o_ref[h * span // LANES + tile, pl.ds(t, count, stride=STEP), :] = turned[
                    h * HALF + AHEAD : h * HALF + AHEAD + count
                ]
    for tile in range(m_count // LANES):
        out_ref[0, :, pl.ds(tile * LANES, LANES)] = o_ref[tile]


JOINT = 8


def sequence_best(contrasts, slopes, q_count, m_count):
    span = m_count // 2
    depth = LEFT + span
    joint = math.gcd(JOINT, slopes.shape[0])
    return pl.pallas_call(
        best_kernel,
        out_shape=jax.ShapeDtypeStruct((1, q_count, m_count), jnp.float32),
        in_specs=[
            pl.BlockSpec(memory_space=pltpu.SMEM),
            pl.BlockSpec(memory_space=pltpu.VMEM),
        ],
        out_specs=pl.BlockSpec(memory_space=pltpu.VMEM),
        scratch_shapes=[
            pltpu.VMEM((STEP, depth, LANES), jnp.float32),
            pltpu.VMEM((STEP - 1, depth, LANES), jnp.float32),
            pltpu.VMEM((STEP, span, LANES), jnp.float32),
            pltpu.VMEM((m_count // LANES, q_count, LANES), jnp.float32),
        ]
        + [pltpu.VMEM((depth, LANES), jnp.float32)] * (joint * (STEP + 1)),
        compiler_params=pltpu.CompilerParams(vmem_limit_bytes=40 << 20),
        name="best",
    )(slopes, contrasts)


def solution(mesh):
    npb, nma = mesh.shape["pb"], mesh.shape["ma"]

    def local(queries, map_descriptors, slopes):
        q_count, m_count = queries.shape[1] * nma, map_descriptors.shape[0]
        queries = pltpu.with_memory_space_constraint(queries, pltpu.HBM)
        map_descriptors = pltpu.with_memory_space_constraint(map_descriptors, pltpu.HBM)
        contrasts = score_tile(queries, map_descriptors, npb, nma)
        return sequence_best(contrasts, slopes, q_count, m_count)

    return jax.shard_map(
        local,
        mesh=mesh,
        in_specs=(P(None, ("pb", "ma"), None), P("ma", "pb"), P()),
        out_specs=P(None, "pb", "ma"),
        check_vma=False,
    )
```

```python
import math

import jax
import jax.numpy as jnp
from jax import lax
from jax.experimental import pallas as pl
from jax.experimental.pallas import tpu as pltpu
from jax.sharding import PartitionSpec as P

MESH = pl.DeviceIdType.MESH
SEQ = 20
RAD = 10
LEAD = 32
LEFT = 384
RIGHT = 128
LANES = 128
CORES = 2
STEP = 5
AHEAD = 8
HALF = 64
LAG = 3


def remote(src, dst, send, recv, where):
    return pltpu.make_async_remote_copy(
        src_ref=src,
        dst_ref=dst,
        send_sem=send,
        recv_sem=recv,
        device_id=where,
        device_id_type=MESH,
    )


def coded(block, narrow=True):
    top = jnp.max(jnp.abs(block), axis=1, keepdims=True)
    power = jnp.ceil(jnp.log2(jnp.maximum(top, 1e-30)) + 1e-3)
    code = jnp.floor(block * jnp.exp2(15.0 - power) + 0.5)
    code = jnp.clip(code, -32767.0, 32767.0)
    tail = jnp.broadcast_to(power, (block.shape[0], LANES))
    code, tail = code.astype(jnp.int32), tail.astype(jnp.int32)
    return (code.astype(jnp.int16), tail.astype(jnp.int16)) if narrow else (code, tail)


def band_of(depth, width, lead):
    inner = lax.broadcasted_iota(jnp.int32, (depth, width), 0)
    outer = lax.broadcasted_iota(jnp.int32, (depth, width), 1)
    near = jnp.abs(inner - lead - outer) <= RAD
    return jnp.where(near, 1.0, 0.0).astype(jnp.bfloat16)


def windows(value, band):
    terms = []
    for item in (value, value * value):
        high = item.astype(jnp.bfloat16)
        terms += [high, (item - high.astype(jnp.float32)).astype(jnp.bfloat16)]
    total = jnp.dot(
        jnp.concatenate(terms, axis=0), band, preferred_element_type=jnp.float32
    )
    rows = value.shape[0]
    part = [total[n * rows : (n + 1) * rows] for n in range(4)]
    scale = 1.0 / (2 * RAD + 1)
    return (part[0] + part[1]) * scale, (part[2] + part[3]) * scale


def whole(code):
    return code.astype(jnp.int32).astype(jnp.float32)


def score_kernel(
    npb,
    nma,
    q_ref,
    m_ref,
    c_ref,
    out_ref,
    q_all,
    m_all,
    p_out,
    p_in,
    r_out,
    l_out,
    l_in,
    r_in,
    local_sem,
    m_send,
    m_recv,
    y_send,
    y_recv,
    z_send,
    z_recv,
    x_send,
    x_recv,
    p_send,
    p_recv,
    halo_send,
    halo_recv,
    lead_send,
    lead_recv,
):
    pb, ma = lax.axis_index("pb"), lax.axis_index("ma")
    pair, across = npb // CORES, nma // 2
    row, core = pb // CORES, pb % CORES
    z, x = ma // 2, ma % 2
    each = q_all.shape[2]
    share = q_all.shape[3]
    m_count, half = m_ref.shape
    size = 2 * each
    last = across - 1
    mate = {"pb": row * CORES + 1 - core}
    twin = {"ma": z * 2 + 1 - x}
    block_of = [lax.rem(row + pair - k, pair) for k in range(pair)]
    row_at = [{"pb": lax.rem(row + k, pair) * CORES + core} for k in range(pair)]
    below, above = {"ma": ma - 2}, {"ma": ma + 2}
    has_below, has_above = z > 0, z < last
    has_up, has_down = pb > 0, pb < npb - 1
    offset = STEP * AHEAD - LEAD
    tiles = c_ref.shape[0]
    has_left, has_right = ma > 0, ma < nma - 1

    barrier = pltpu.get_barrier_semaphore()

    def greet(where):
        pl.semaphore_signal(barrier, inc=1, device_id=where, device_id_type=MESH)

    greet(mate)
    greet(twin)
    for k in range(1, pair):
        greet(row_at[k])
    sides = (
        (has_above, above),
        (has_below, below),
        (has_left, {"ma": ma - 1}),
        (has_right, {"ma": ma + 1}),
        (has_up, {"pb": pb - 1}),
        (has_down, {"pb": pb + 1}),
        (has_up & has_left, {"pb": pb - 1, "ma": ma - 1}),
        (has_up & has_right, {"pb": pb - 1, "ma": ma + 1}),
        (has_down & has_left, {"pb": pb + 1, "ma": ma - 1}),
        (has_down & has_right, {"pb": pb + 1, "ma": ma + 1}),
    )
    for test, where in sides:

        @pl.when(test)
        def _():
            greet(where)

    extra = sum(jnp.where(test, 1, 0) for test, _ in sides)
    pl.semaphore_wait(barrier, pair + 1 + extra)

    def part(k):
        at = pl.multiple_of(lax.rem(row + k, pair) * share, LANES)
        return q_ref.at[0, :, pl.ds(at, share)]

    to_row = [None] + [
        remote(part(k), q_all.at[row, ma], y_send.at[k], y_recv.at[k], row_at[k])
        for k in range(1, pair)
    ]
    for copy in to_row[1:]:
        copy.start()
    load_q = pltpu.make_async_copy(part(0), q_all.at[row, ma], local_sem.at[0])
    load_q.start()
    to_mate = remote(m_ref, m_all.at[core], m_send.at[0], m_recv.at[0], mate)
    to_mate.start()
    load_m = pltpu.make_async_copy(m_ref, m_all.at[core], local_sem.at[1])
    load_m.start()

    def ranked(e):
        far = lax.div(e + 1, 2)
        there = z + jnp.where(lax.rem(e, 2) == 1, -far, far)
        return there, (there >= 0) & (there <= last)

    def block_at(k, there, column):
        return q_all.at[block_of[k], there * 2 + column]

    def along_z(k, there, number, where):
        block = block_at(k, there, x)
        return remote(block, block, z_send.at[k, number], z_recv.at[k, there], where)

    def along_x(k, there):
        block = block_at(k, there, x)
        return remote(block, block, x_send.at[k, there], x_recv.at[k, there], twin)

    def spread(k):
        along_x(k, z).start()

        @pl.when(has_above)
        def _():
            along_z(k, z, z, above).start()

        @pl.when(has_below)
        def _():
            along_z(k, z, across, below).start()

    def forward(k, e):
        there, known = ranked(e)

        @pl.when(known)
        def _():
            along_z(k, there, there, twin).wait_recv()
            along_x(k, there).start()

        @pl.when(known & (there < z) & has_above)
        def _():
            along_z(k, there, there, above).start()

        @pl.when(known & (there > z) & has_below)
        def _():
            along_z(k, there, there, below).start()

    def from_x(k, there):
        block = block_at(k, there, 1 - x)
        return remote(block, block, x_send.at[k, there], x_recv.at[k, there], twin)

    load_q.wait()
    spread(0)
    forward(0, 1)
    forward(0, 2)
    for k in range(1, pair):
        to_row[k].wait_recv()
        spread(k)

    load_m.wait()
    to_mate.wait_recv()

    @pl.when(pb == 0)
    def _():
        c_ref[:, pl.ds(offset, LEAD), :] = jnp.zeros((tiles, LEAD, LANES), jnp.float32)

    @pl.when(ma == 0)
    def _():
        out_ref[:, pl.ds(0, LEFT)] = jnp.zeros((out_ref.shape[0], LEFT), jnp.float32)

    @pl.when(ma == nma - 1)
    def _():
        out_ref[:, pl.ds(LEFT + m_count, RIGHT)] = jnp.zeros(
            (out_ref.shape[0], RIGHT), jnp.float32
        )

    def score(k, there):
        block = q_all[block_of[k], pl.ds(there * 2, 2)]
        if each % 16 == 0:
            block = block.reshape(size, share)
        else:
            block = block.astype(jnp.float32).reshape(size, share).astype(block.dtype)
        total = None
        for slot in range(CORES):
            term = lax.dot_general(
                block[:, slot * half : (slot + 1) * half],
                m_all[slot],
                (((1,), (1,)), ((), ())),
                preferred_element_type=jnp.float32,
            )
            total = term if total is None else total + term
        return total

    def partial(k, there):
        return remote(
            p_out.at[k - 1, there],
            p_in.at[k - 1, there],
            p_send.at[k - 1, there],
            p_recv.at[k - 1, there],
            row_at[pair - k],
        )

    def add_partials(e):
        there, known = ranked(e)
        for k in range(1, pair):

            @pl.when(known)
            def _():
                from_x(k, there).wait_recv()
                code, tail = coded(score(k, there))
                p_out[k - 1, there, :, pl.ds(0, m_count)] = code
                p_out[k - 1, there, :, pl.ds(m_count, LANES)] = tail
                partial(k, there).start()

    lead_each = min(LEAD, size)
    lead_parts = LEAD // lead_each

    def halos(there):
        right = remote(
            r_out.at[there], l_in.at[there], halo_send.at[0, there], halo_recv.at[0, there],
            {"ma": ma + 1},
        )
        left = remote(
            l_out.at[there], r_in.at[there], halo_send.at[1, there], halo_recv.at[1, there],
            {"ma": ma - 1},
        )
        return (has_right, has_left, right), (has_left, has_right, left)

    def leads(number):
        there = across - lead_parts + number
        rows = pl.ds(size - lead_each, lead_each)
        into = pl.ds(number * lead_each, lead_each)
        slot = across + number
        down, up = has_down, has_up
        main = remote(
            out_ref.at[pl.ds(LEAD + (there + 1) * size - lead_each, lead_each), pl.ds(LEFT, m_count)],
            out_ref.at[into, pl.ds(LEFT, m_count)],
            lead_send.at[0, number], lead_recv.at[0, number], {"pb": pb + 1},
        )
        right = remote(
            r_out.at[there, rows], l_in.at[slot, pl.ds(0, lead_each)],
            lead_send.at[1, number], lead_recv.at[1, number], {"pb": pb + 1, "ma": ma + 1},
        )
        left = remote(
            l_out.at[there, rows], r_in.at[slot, pl.ds(0, lead_each)],
            lead_send.at[2, number], lead_recv.at[2, number], {"pb": pb + 1, "ma": ma - 1},
        )
        return (
            (down, up, main),
            (down & has_right, up & has_left, right),
            (down & has_left, up & has_right, left),
        )

    def start(group):
        for sends, _, copy in group:

            @pl.when(sends)
            def _():
                copy.start()

    def edged(block, spare):
        code, tail = coded(block, narrow=False)
        lane = lax.broadcasted_iota(jnp.int32, code.shape, 1)
        if code.shape[1] > LANES:
            tail = jnp.concatenate([tail] * (code.shape[1] // LANES), axis=1)
        return jnp.where((lane >= spare) & (lane < spare + 16), tail, code).astype(jnp.int16)

    def opened(code, spare):
        value = whole(code)
        return value * jnp.exp2(value[:, spare : spare + 1] - 15.0)

    edge = band_of(2 * LANES, LANES, 0)
    inside = band_of(4 * LANES, 2 * LANES, LANES)

    def contrast(at, count, tile, lead, band):
        value = out_ref[pl.ds(at, count), pl.ds(tile * LANES - lead, band.shape[0])]
        width = band.shape[1]
        centre = value[:, lead : lead + width]
        average, square = windows(value, band)
        spread = square - average * average
        normal = (centre - average) * (
            lax.rsqrt(spread + 1.0) * (1.0 / math.sqrt(SEQ))
        )
        for side in range(width // LANES):
            part = normal[:, side * LANES : (side + 1) * LANES]
            if tile + side < LEFT // LANES:
                part = jnp.where(ma == 0, 0.0, part)
            c_ref[tile + side, pl.ds(at + offset, count), :] = part

    inner_tiles = range(LEFT // LANES + 2, tiles - 2, 2)
    outer_tiles = [t for t in range(1, tiles, 2) if t not in inner_tiles]

    def outer(at, count):
        contrast(at, count, 0, 0, edge)
        for tile in outer_tiles:
            contrast(at, count, tile, LANES, inside)

    def own(e):
        there, known = ranked(e)

        @pl.when(known)
        def _():
            from_x(0, there).wait_recv()
            total = score(0, there)
            for k in range(1, pair):
                partial(k, there).wait_recv()
                scale = jnp.exp2(whole(p_in[k - 1, there, :, pl.ds(m_count, LANES)]) - 15.0)
                code = whole(p_in[k - 1, there, :, pl.ds(0, m_count)])
                total = total + code * scale[:, :1]
            at = pl.multiple_of(LEAD + there * size, 8)
            out_ref[pl.ds(at, size), pl.ds(LEFT, m_count)] = total
            r_out[there] = edged(total[:, m_count - LEFT :], 0)
            l_out[there] = edged(total[:, :RIGHT], LANES - 16)
            start(halos(there))
            for number in range(lead_parts):

                @pl.when(there == across - lead_parts + number)
                def _():
                    start(leads(number))

            for tile in inner_tiles:
                contrast(at, size, tile, LANES, inside)

    def finish(group):
        for sends, receives, copy in group:

            @pl.when(receives)
            def _():
                copy.wait_recv()

            @pl.when(sends)
            def _():
                copy.wait_send()

    def unpack(rows, slot, count):
        @pl.when(has_left)
        def _():
            out_ref[rows, pl.ds(0, LEFT)] = opened(l_in[slot, pl.ds(0, count)], 0)

        @pl.when(has_right)
        def _():
            out_ref[rows, pl.ds(LEFT + m_count, RIGHT)] = opened(
                r_in[slot, pl.ds(0, count)], LANES - 16
            )

    def outline(e):
        there, known = ranked(e)

        @pl.when(known)
        def _():
            finish(halos(there))
            at = pl.multiple_of(LEAD + there * size, 8)
            unpack(pl.ds(at, size), there, size)
            outer(at, size)

    def at_distance(d, act):
        @pl.when(d >= 0)
        def _():
            @pl.when(d > 0)
            def _():
                act(2 * d - 1)

            act(2 * d)

    @pl.loop(0, across + 2 * LAG)
    def _(d):
        for e in (2 * d + 1, 2 * d + 2):
            for k in range(1, pair):
                forward(k, e)

        @pl.when(d > 1)
        def _():
            for e in (2 * d - 1, 2 * d):
                forward(0, e)

        at_distance(d, add_partials)
        at_distance(d - LAG, own)
        at_distance(d - 2 * LAG, outline)

    @pl.loop(0, 2 * across - 1)
    def _(e):
        there, known = ranked(e)

        @pl.when(known)
        def _():
            for k in range(1, pair):
                partial(k, there).wait_send()
            for k in range(pair):
                along_x(k, there).wait_send()

        onward = ((there < z) & has_above) | ((there > z) & has_below)
        for k in range(pair):

            @pl.when(known & onward)
            def _():
                along_z(k, there, there, twin).wait_send()

    for number in range(lead_parts):
        finish(leads(number))

        @pl.when(has_up)
        def _():
            unpack(pl.ds(number * lead_each, lead_each), across + number, lead_each)
            for tile in inner_tiles:
                contrast(number * lead_each, lead_each, tile, LANES, inside)
            outer(number * lead_each, lead_each)

    for k in range(1, pair):
        to_row[k].wait_send()
    to_mate.wait_send()
    for k in range(pair):

        @pl.when(has_above)
        def _():
            along_z(k, z, z, above).wait_send()

        @pl.when(has_below)
        def _():
            along_z(k, z, across, below).wait_send()


def score_tile(queries, map_descriptors, npb, nma):
    each, width = queries.shape[1:]
    m_count, half = map_descriptors.shape
    q_count = each * nma
    pair, across = npb // CORES, nma // 2
    size = 2 * each
    parts = LEAD // min(LEAD, size)
    dma = pltpu.SemaphoreType.DMA
    return pl.pallas_call(
        lambda *refs: score_kernel(npb, nma, *refs),
        out_shape=jax.ShapeDtypeStruct(
            ((LEFT + m_count) // LANES, STEP * HALF, LANES), jnp.float32
        ),
        in_specs=[pl.BlockSpec(memory_space=pltpu.HBM)] * 2,
        out_specs=pl.BlockSpec(memory_space=pltpu.VMEM),
        scratch_shapes=[
            pltpu.VMEM((LEAD + q_count, LEFT + m_count + RIGHT), jnp.float32),
            pltpu.VMEM((pair, nma, each, width // pair), jnp.bfloat16),
            pltpu.VMEM((CORES, m_count, half), jnp.bfloat16),
            pltpu.VMEM((pair - 1, across, size, m_count + LANES), jnp.int16),
            pltpu.VMEM((pair - 1, across, size, m_count + LANES), jnp.int16),
            pltpu.VMEM((across, size, LEFT), jnp.int16),
            pltpu.VMEM((across, size, RIGHT), jnp.int16),
            pltpu.VMEM((across + parts, size, LEFT), jnp.int16),
            pltpu.VMEM((across + parts, size, RIGHT), jnp.int16),
            dma((2,)),
            dma((1,)),
            dma((1,)),
            dma((pair,)),
            dma((pair,)),
            dma((pair, across + 1)),
            dma((pair, across)),
            dma((pair, across)),
            dma((pair, across)),
            dma((pair - 1, across)),
            dma((pair - 1, across)),
            dma((2, across)),
            dma((2, across)),
            dma((3, across)),
            dma((3, across)),
        ],
        compiler_params=pltpu.CompilerParams(
            collective_id=0, has_side_effects=True, vmem_limit_bytes=32 << 20
        ),
        name="scores",
    )(queries, map_descriptors)


def best_kernel(slopes_ref, c_ref, out_ref, u_ref, w_ref, b_ref, o_ref, *scratch):
    q_count, m_count = out_ref.shape[1:]

    span = m_count // 2
    depth = LEFT + span
    for t in range(STEP):
        for tile in range(depth // LANES):
            both = [
                c_ref[h * span // LANES + tile, pl.ds(t, HALF, stride=STEP), :]
                for h in range(2)
            ]
            turned = jnp.transpose(jnp.concatenate(both, axis=0))
            at = pl.ds(tile * LANES, LANES)
            u_ref[t, at, :] = turned
            if t < STEP - 1:
                w_ref[t, at, :] = pltpu.roll(turned, SEQ // STEP, 1)

    start = LEFT - 288, LEFT - 216, LEFT - 64, LEFT - 48, LEFT - 32, LEFT - 16, LEFT

    def vec(at):
        return pl.ds(at, 8)

    joint = len(scratch) // (STEP + 1)
    once = joint == slopes_ref.shape[0]
    if not once:
        b_ref[...] = jnp.full(b_ref.shape, -jnp.inf, jnp.float32)
    stages = [scratch[n * (STEP + 1) : (n + 1) * (STEP + 1)] for n in range(joint)]

    @pl.loop(0, slopes_ref.shape[0] // joint)
    def _(index):
        known = [(slopes_ref[index * joint + n], *stages[n]) for n in range(joint)]
        for at in range(start[0], depth, 8):
            here = u_ref[STEP - 1, vec(at), :]
            for v, f_ref, *_ in known:
                total = here
                for k in range(1, STEP):
                    total = total + u_ref[STEP - 1 - k, vec(at - k * v), :]
                f_ref[vec(at), :] = total
        for at in range(start[1], depth, 8):
            for v, f_ref, g_ref, *_ in known:
                g_ref[vec(at), :] = f_ref[vec(at), :] + pltpu.roll(
                    f_ref[vec(at - STEP * v), :], 1, 1
                )
        for at in range(start[2], depth, 8):
            into = vec(at - LEFT)
            best = None if once or at < LEFT else b_ref[STEP - 1, into, :]
            for v, _, g_ref, s_ref, *_ in known:
                total = g_ref[vec(at), :] + pltpu.roll(
                    g_ref[vec(at - 2 * STEP * v), :], 2, 1
                )
                s_ref[vec(at), :] = total
                best = total if best is None else jnp.maximum(best, total)
            if at >= LEFT:
                b_ref[STEP - 1, into, :] = best
        for t in range(STEP - 1):
            for at in range(start[3 + t], depth, 8):
                into = vec(at - LEFT)
                best = None if once or at < LEFT else b_ref[t, into, :]
                here = u_ref[t, vec(at), :]
                for v, _, _, *s_refs in known:
                    before = s_refs[t][vec(at - v), :]
                    if t == 0:
                        before = pltpu.roll(before, 1, 1)
                    total = before + (here - w_ref[t, vec(at - SEQ * v), :])
                    if t < STEP - 2:
                        s_refs[t + 1][vec(at), :] = total
                    best = total if best is None else jnp.maximum(best, total)
                if at >= LEFT:
                    b_ref[t, into, :] = best

    for tile in range(span // LANES):
        for t in range(STEP):
            count = (q_count - t + STEP - 1) // STEP
            turned = jnp.transpose(b_ref[t, pl.ds(tile * LANES, LANES), :])
            for h in range(2):
                o_ref[h * span // LANES + tile, pl.ds(t, count, stride=STEP), :] = turned[
                    h * HALF + AHEAD : h * HALF + AHEAD + count
                ]
    for tile in range(m_count // LANES):
        out_ref[0, :, pl.ds(tile * LANES, LANES)] = o_ref[tile]


JOINT = 8


def sequence_best(contrasts, slopes, q_count, m_count):
    span = m_count // 2
    depth = LEFT + span
    joint = math.gcd(JOINT, slopes.shape[0])
    return pl.pallas_call(
        best_kernel,
        out_shape=jax.ShapeDtypeStruct((1, q_count, m_count), jnp.float32),
        in_specs=[
            pl.BlockSpec(memory_space=pltpu.SMEM),
            pl.BlockSpec(memory_space=pltpu.VMEM),
        ],
        out_specs=pl.BlockSpec(memory_space=pltpu.VMEM),
        scratch_shapes=[
            pltpu.VMEM((STEP, depth, LANES), jnp.float32),
            pltpu.VMEM((STEP - 1, depth, LANES), jnp.float32),
            pltpu.VMEM((STEP, span, LANES), jnp.float32),
            pltpu.VMEM((m_count // LANES, q_count, LANES), jnp.float32),
        ]
        + [pltpu.VMEM((depth, LANES), jnp.float32)] * (joint * (STEP + 1)),
        compiler_params=pltpu.CompilerParams(vmem_limit_bytes=40 << 20),
        name="best",
    )(slopes, contrasts)


def solution(mesh):
    npb, nma = mesh.shape["pb"], mesh.shape["ma"]

    def local(queries, map_descriptors, slopes):
        q_count, m_count = queries.shape[1] * nma, map_descriptors.shape[0]
        queries = pltpu.with_memory_space_constraint(queries, pltpu.HBM)
        map_descriptors = pltpu.with_memory_space_constraint(map_descriptors, pltpu.HBM)
        contrasts = score_tile(queries, map_descriptors, npb, nma)
        return sequence_best(contrasts, slopes, q_count, m_count)

    return jax.shard_map(
        local,
        mesh=mesh,
        in_specs=(P(None, ("pb", "ma"), None), P("ma", "pb"), P()),
        out_specs=P(None, "pb", "ma"),
        check_vma=False,
    )
```
